32 devices in a mesh: gx: 8 (over z, y), sec: 4 (over x, core).
Axes of the slice: x: 2, y: 2, z: 4, core: 2. Of those that a mesh axis runs over, the one named last changes fastest.
Arguments:
- scalar_field: float32 [8, 128, 4096], P(None, 'gx', 'sec'), may hold values from -6 to 6
- diffusivity: float32 [8, 128, 4096], P(None, 'gx', 'sec'), may hold values from 0.02 to 0.16
- corner_x: int32 [8, 4, 4], P('gx', 'sec'), may hold values from 0 to 15
- corner_y: int32 [8, 4, 4], P(None, 'sec'), may hold values from 0 to 1016
- patch_owner: int32 [8, 4, 4], P('gx'), may hold values from 0 to 3, as said below
- lift_weight: float32 [64, 54], replicated, may hold values from -0.875 to 0.875
- mix_weight: float32 [64, 1728], replicated, may hold values from -0.15625 to 0.15625
- out_weight: float32 [1, 64], replicated, may hold values from -0.75 to 0.75
Outputs:
- advanced: float32 [8, 128, 4096], P(None, 'gx', 'sec')
- lift_grad: float32 [64, 54], replicated
- mix_grad: float32 [64, 1728], replicated
- out_grad: float32 [1, 64], replicated
- trainer_loss: float32 [8, 4], P('gx', 'sec')
The draws below stay inside these ranges and needn't reach their ends.
Inputs may be any that keep to these rules, and one draw needn't show every extreme that they name: `patch_owner`: owners are trainers of the patch's own row. At most 2 patches of one block share an owner, and in every block 2 do. In every row one trainer owns exactly 8 patches.
All inputs are finite; a program needn't handle non-finite values.
Results may differ from the reference program's by a relative error of at most 0.0003.
Values sent between devices are 32-bit elements; how exact they have to be, the bound alone decides.
A program may use at most 64 MiB of HBM per device.

```python
import math
import jax
import jax.numpy as jnp
from jax import lax

C = 64
NZ = 8
CX = 16
CY = 1024
PS = 4
COLUMNS = 4
ROWS = 8
NX = 128
NY = 4096


def draw_patch_owner(key, part):

    def one_row(number):
        row_key = jax.random.fold_in(key, number)
        order = jax.random.permutation(jax.random.fold_in(row_key, 7), COLUMNS).astype(jnp.int32)
        busiest = order[0]
        others = order[1:]
        rest = COLUMNS - 1

        def one_source(source):
            first = others[source % rest]
            second = others[(source + 1) % rest]
            listed = jnp.stack([busiest, busiest, first, second]).astype(jnp.int32)
            shuffle = jax.random.permutation(jax.random.fold_in(row_key, 100 + source), PS)
            return listed[shuffle].astype(jnp.int32)
        return jax.vmap(one_source)(jnp.arange(COLUMNS, dtype=jnp.int32))
    return jax.vmap(one_row)(jnp.arange(ROWS, dtype=jnp.int32))


def with_ends(array, rng, smallest, top_value):
    longest = array.shape.index(max(array.shape))
    spots = []
    for shift in (0, 1):
        where = [jax.random.randint(jax.random.fold_in(rng, axis), (), 0, length) for axis, length in enumerate(array.shape)]
        where[longest] = (where[longest] + shift) % array.shape[longest]
        spots.append(tuple(where))
    return array.at[spots[0]].set(smallest).at[spots[1]].set(top_value)


def levels(own_key, shape, pieces, low, top_value):
    factor_of, own = 1.0, jax.random.fold_in(own_key, 6)
    for axis_at, shards_of in pieces:
        draws = jnp.exp(jax.random.uniform(jax.random.fold_in(own, axis_at), (shards_of,), jnp.float32, low / len(pieces), top_value / len(pieces)))
        factor_of = factor_of * jnp.repeat(draws, shape[axis_at] // shards_of).reshape([-1 if axis == axis_at else 1 for axis in range(len(shape))])
    return factor_of


def centred(own_key, extent, spread, reach, pieces=(), held_as=jnp.bfloat16):
    values = spread * jax.random.normal(own_key, extent, jnp.float32)
    if pieces:
        values = values * levels(own_key, extent, pieces, -0.22, 0.18)
    return jnp.clip(values, -reach, reach).astype(held_as)


def setup_inputs(seed: int = 0) -> dict:
    splits = jax.random.split(jax.random.key(seed), 9)
    scalar_field = centred(splits[0], (NZ, NX, NY), 1.0, 6.0, ((1, 8), (2, 4)), jnp.float32)
    diffusivity = jnp.clip(jnp.exp(math.log(0.16) - 2.0794415 * jax.random.uniform(splits[1], (NZ, NX, NY), jnp.float32) ** levels(splits[1], (NZ, NX, NY), ((1, 8), (2, 4)), -0.2, 0.2)), 0.02, 0.16)
    corner_x = with_ends(jax.random.randint(splits[2], (ROWS, COLUMNS, PS), 0, CX), jax.random.fold_in(splits[2], 1), 0, CX - 1).astype(jnp.int32)
    corner_y = with_ends(jax.random.randint(splits[3], (ROWS, COLUMNS, PS), 0, CY - NZ + 1), jax.random.fold_in(splits[3], 1), 0, CY - NZ).astype(jnp.int32)
    patch_owner = draw_patch_owner(jax.random.fold_in(splits[8], 71), 0)
    lift_weight = centred(splits[5], (C, 54), 54 ** -0.5, 0.875, (), jnp.float32)
    mix_weight = centred(splits[6], (C, 27 * C), (27 * C) ** -0.5, 0.15625, (), jnp.float32)
    out_weight = centred(splits[7], (1, C), C ** -0.5, 0.75, (), jnp.float32)
    return dict(scalar_field=scalar_field, diffusivity=diffusivity, corner_x=corner_x, corner_y=corner_y, patch_owner=patch_owner, lift_weight=lift_weight, mix_weight=mix_weight, out_weight=out_weight)


HIGHEST_PRECISION = lax.Precision.HIGHEST

def advance(extended, factor):
    center = extended[:, 1:-1, 1:-1]
    z_padded = jnp.pad(center, ((1, 1), (0, 0), (0, 0)))
    beside = extended[:, 2:, 1:-1] + extended[:, :-2, 1:-1]
    beside = beside + extended[:, 1:-1, 2:] + extended[:, 1:-1, :-2]
    beside = beside + z_padded[2:] + z_padded[:-2]
    return center + factor * (beside - 6.0 * center)

def diffuse(values, factor):
    return advance(jnp.pad(values, ((0, 0), (1, 1), (1, 1))), factor)

def convolve(inputs, kernel):
    return lax.conv_general_dilated(inputs, kernel, (1, 1, 1), 'SAME', dimension_numbers=('NCDHW', 'OIDHW', 'NCDHW'), precision=HIGHEST_PRECISION)

def patch_errors(lift_weight, mix_weight, out_weight, inputs, target):
    channels = mix_weight.shape[0]
    hidden = jax.nn.silu(convolve(inputs, lift_weight.reshape(channels, 2, 3, 3, 3)))
    hidden = jax.nn.silu(convolve(hidden, mix_weight.reshape(channels, channels, 3, 3, 3)))
    predicted = jnp.einsum('c,bczxy->bzxy', out_weight[0], hidden, precision=HIGHEST_PRECISION)
    misfit = predicted - target
    return lax.optimization_barrier(jnp.mean(misfit * misfit, axis=(1, 2, 3)))

def train_grads(lift_weight, mix_weight, out_weight, stacked, cotangent):

    def loss_of(first, second, third):
        return patch_errors(first, second, third, stacked[:, 0:2], stacked[:, 2])
    errors, pullback = jax.vjp(loss_of, lift_weight, mix_weight, out_weight)
    gradients = pullback(cotangent.astype(errors.dtype))
    return (errors, gradients)

def reference(scalar_field, diffusivity, corner_x, corner_y, patch_owner, lift_weight, mix_weight, out_weight):
    first_step = diffuse(scalar_field, diffusivity)
    advanced = diffuse(first_step, diffusivity)
    change = advanced - first_step
    fields = jnp.stack([first_step, diffusivity, change])
    padded = jnp.pad(fields, ((0, 0), (0, 0), (0, NZ), (0, 0)))
    weight = 1.0 / PS

    def one_row(carry, number):
        corners_x = lax.dynamic_index_in_dim(corner_x, number, 0, keepdims=False).reshape(-1)
        corners_y = lax.dynamic_index_in_dim(corner_y, number, 0, keepdims=False).reshape(-1)
        owners = lax.dynamic_index_in_dim(patch_owner, number, 0, keepdims=False).reshape(-1)
        column_ids = jnp.arange(COLUMNS * PS, dtype=jnp.int32) // PS
        x_starts = (number * CX + corners_x).astype(jnp.int32)
        y_starts = (column_ids * CY + corners_y).astype(jnp.int32)

        def take(x_start, y_start):
            zero = jnp.zeros((), jnp.int32)
            return lax.dynamic_slice(padded, (zero, zero, x_start, y_start), (3, NZ, NZ, NZ))
        stacked = jax.vmap(take)(x_starts, y_starts)
        cotangent = jnp.full((COLUMNS * PS,), weight, jnp.float32)
        errors, gradients = train_grads(lift_weight, mix_weight, out_weight, stacked, cotangent)
        member = owners[None, :] == jnp.arange(COLUMNS, dtype=jnp.int32)[:, None]
        per_trainer = lax.optimization_barrier(jnp.sum(jnp.where(member, errors[None, :], jnp.zeros((), errors.dtype)), axis=1))
        carry = jax.tree.map(lambda left, right: left + right, carry, gradients)
        return (carry, per_trainer)
    start = (jnp.zeros_like(lift_weight), jnp.zeros_like(mix_weight), jnp.zeros_like(out_weight))
    totals, losses = lax.scan(one_row, start, jnp.arange(ROWS, dtype=jnp.int32))
    return (advanced, totals[0], totals[1], totals[2], losses)
```

```python
import functools

import jax
import jax.numpy as jnp
from jax import lax
from jax.experimental import pallas as pl
from jax.experimental.pallas import tpu as pltpu
from jax.sharding import PartitionSpec as P

MESH = pl.DeviceIdType.MESH
F32 = jnp.float32
BF16 = jnp.bfloat16
LANES = 128
SUBLANES = 8
LIFT_AT = 576
PACKED = 640


def padded(cells, sides, width):
    for axis, dim in sides:
        count = lax.axis_size(axis)
        ends = count - 1
        head = lax.slice_in_dim(cells, 0, width, axis=dim)
        tail = lax.slice_in_dim(cells, cells.shape[dim] - width, cells.shape[dim], axis=dim)
        cells = jnp.concatenate(
            [
                lax.ppermute(tail, axis, [(i, (i + 1) % count) for i in range(ends)]),
                cells,
                lax.ppermute(head, axis, [((i + 1) % count, i) for i in range(ends)]),
            ],
            axis=dim,
        )
    return cells


def from_behind(value, axis, by):
    size = lax.axis_size(axis)
    pairs = [(i, i + by) for i in range(size) if 0 <= i + by < size]
    return lax.ppermute(value, axis, pairs)


def advance(extended, factor):
    center = extended[:, 1:-1, 1:-1]
    z_padded = jnp.pad(center, ((1, 1), (0, 0), (0, 0)))
    beside = extended[:, 2:, 1:-1] + extended[:, :-2, 1:-1]
    beside = beside + extended[:, 1:-1, 2:] + extended[:, 1:-1, :-2]
    beside = beside + z_padded[2:] + z_padded[:-2]
    return center + factor * (beside - 6.0 * center)


def split(values):
    high = values.astype(BF16)
    return high, (values - high.astype(F32)).astype(BF16)


def product(high, low, other_high, other_low, contract):
    dims = (contract, ((), ()))
    dot = functools.partial(lax.dot_general, dimension_numbers=dims, preferred_element_type=F32)
    return dot(high, other_high) + (dot(low, other_high) + dot(high, other_low))


def lift_row(tap):
    return tap * 8 if tap < 5 else (tap - 5) * 8 + 4


def surrogate_kernel(
    owners, fields, target, lift, mix, mix_back, out_w, packed,
    lift_high, lift_low, taps_high, taps_low, back_high, back_low, mixed,
    first_slope, grad_high, grad_low,
):
    depth = 8
    tiles = fields.shape[1] // LANES
    channels = out_w.shape[0]
    lane = lax.broadcasted_iota(jnp.int32, (1, LANES), 1)
    x_at, y_at = (lane // 8) % 8, lane % 8
    masks = []
    for tap in range(9):
        dx, dy = tap // 3 - 1, tap % 3 - 1
        masks.append(
            (x_at + dx >= 0) & (x_at + dx < 8) & (y_at + dy >= 0) & (y_at + dy < 8)
        )

    def shifted(values, tap):
        step = (tap // 3 - 1) * 8 + tap % 3 - 1
        moved = pltpu.roll(values, (-step) % LANES, 1) if step else values
        return jnp.where(masks[tap], moved, 0.0)

    def cols(k):
        return slice(k * LANES, (k + 1) * LANES)

    lift_high[...] = jnp.zeros_like(lift_high)
    lift_low[...] = jnp.zeros_like(lift_low)
    for k in range(tiles):
        lower, upper = fields[0:8, cols(k)], fields[8:16, cols(k)]
        blocks = []
        for at in range(5):
            block = shifted(lower, at)
            if at < 4:
                block = block + shifted(upper, at + 5)
            blocks.append(block)
        blocks.append(jnp.zeros_like(lower))
        high, low = split(jnp.concatenate(blocks, axis=0))
        lift_high[64:112, cols(k)] = high
        lift_low[64:112, cols(k)] = low

    def gathered(k):
        z = k % depth
        total = mixed[channels : 2 * channels, cols(k)]
        if z > 0:
            total = total + mixed[0:channels, cols(k - 1)]
        if z < depth - 1:
            total = total + mixed[2 * channels : 3 * channels, cols(k + 1)]
        return total

    weight_high, weight_low = split(lift[...])
    wide = 2 * LANES
    for at in range(0, tiles * LANES, wide):
        mixed[:, at : at + wide] = product(
            weight_high, weight_low,
            lift_high[64:112, at : at + wide], lift_low[64:112, at : at + wide],
            ((1,), (0,)),
        )
    taps_high[LIFT_AT:, :] = jnp.zeros((PACKED - LIFT_AT, tiles * LANES), BF16)
    taps_low[LIFT_AT:, :] = jnp.zeros((PACKED - LIFT_AT, tiles * LANES), BF16)

    def spread_taps(values, high_ref, low_ref, k):
        for tap in range(9):
            high, low = split(shifted(values, tap))
            high_ref[tap * channels : (tap + 1) * channels, cols(k)] = high
            low_ref[tap * channels : (tap + 1) * channels, cols(k)] = low

    for k in range(tiles):
        pre = gathered(k)
        gate = 1.0 / (1.0 + jnp.exp(-pre))
        first_slope[:, cols(k)] = gate * (1.0 + pre * (1.0 - gate))
        spread_taps(pre * gate, taps_high, taps_low, k)

    def mixing(weights, high_ref, low_ref):
        weight_high, weight_low = split(weights[...])
        for at in range(0, tiles * LANES, wide):
            mixed[:, at : at + wide] = product(
                weight_high, weight_low,
                high_ref[0:LIFT_AT, at : at + wide], low_ref[0:LIFT_AT, at : at + wide],
                ((1,), (0,)),
            )

    mixing(mix, taps_high, taps_low)

    scale = 2.0 / (depth * 64) / 4.0
    weights = jnp.broadcast_to(out_w[...], (channels, LANES))
    out_sum = jnp.zeros((channels, LANES), F32)
    half = lane < 64
    square = [jnp.zeros((1, LANES), F32) for _ in range(tiles // depth)]

    def store_grad(values, k):
        high, low = split(values)
        z = k % depth
        zero = jnp.zeros_like(high)
        for ref, part in ((grad_high, high), (grad_low, low)):
            ref[channels : 2 * channels, cols(k)] = part
            if z > 0:
                ref[0:channels, cols(k - 1)] = part
            else:
                ref[2 * channels : 3 * channels, cols(k)] = zero
            if z < depth - 1:
                ref[2 * channels : 3 * channels, cols(k + 1)] = part
            else:
                ref[0:channels, cols(k)] = zero

    for k in range(tiles):
        pre = gathered(k)
        gate = 1.0 / (1.0 + jnp.exp(-pre))
        hidden = pre * gate
        predicted = jnp.sum(hidden * weights, axis=0, keepdims=True)
        misfit = predicted - target[0:1, cols(k)]
        square[k // depth] = square[k // depth] + misfit * misfit
        pull = misfit * scale
        out_sum = out_sum + hidden * pull
        grad = weights * pull * (gate * (1.0 + pre * (1.0 - gate)))
        store_grad(grad, k)
        spread_taps(grad, back_high, back_low, k)

    mixing(mix_back, back_high, back_low)
    sections = packed.shape[0]
    per = packed.shape[1] - 1
    rows = 3 * channels

    def put(block, column):
        for r in range(rows // SUBLANES):
            at = column * (rows // SUBLANES) + r
            packed[at // per, at % per] = block[r * SUBLANES : (r + 1) * SUBLANES, :]

    nt = ((1,), (1,))
    for column in range(PACKED // LANES - 1):
        part = slice(column * LANES, (column + 1) * LANES)
        put(product(grad_high[...], grad_low[...], taps_high[part, :], taps_low[part, :], nt), column)
    last = PACKED - LANES
    final = product(grad_high[...], grad_low[...], taps_high[last:, :], taps_low[last:, :], nt)
    for k in range(tiles):
        store_grad(gathered(k) * first_slope[:, cols(k)], k)
    final = final + product(grad_high[...], grad_low[...], lift_high[...], lift_low[...], nt)
    out_column = jnp.sum(out_sum, axis=1, keepdims=True)
    lanes_all = lax.broadcasted_iota(jnp.int32, (channels, LANES), 1)
    out_block = jnp.where(lanes_all == LANES - 1, out_column, 0.0)
    final = final + jnp.concatenate(
        [out_block, jnp.zeros((rows - channels, LANES), F32)], axis=0
    )
    put(final, PACKED // LANES - 1)
    for at in range(rows // SUBLANES * (PACKED // LANES), sections * per):
        packed[at // per, at % per] = jnp.zeros((SUBLANES, LANES), F32)
    errors = []
    for pair in range(tiles // depth):
        for side in (half, ~half):
            total = jnp.sum(jnp.where(side, square[pair], 0.0), axis=1, keepdims=True)
            errors.append(jnp.broadcast_to(total / (depth * 64), (SUBLANES, LANES)))
    for trainer in range(sections):
        mine = jnp.zeros((SUBLANES, LANES), F32)
        for number, error in enumerate(errors):
            mine = mine + jnp.where(owners[number] == trainer, error, 0.0)
        packed[trainer, per] = mine


def surrogate(owners, fields, target, lift, mix, mix_back, out_w, sections, per):
    cells = fields.shape[1]
    channels = out_w.shape[0]
    vmem = pl.BlockSpec(memory_space=pltpu.VMEM)
    wide = pltpu.VMEM((PACKED, cells), BF16)
    return pl.pallas_call(
        surrogate_kernel,
        out_shape=jax.ShapeDtypeStruct((sections, per + 1, SUBLANES, LANES), F32),
        in_specs=[pl.BlockSpec(memory_space=pltpu.SMEM)] + [vmem] * 6,
        out_specs=vmem,
        scratch_shapes=[
            pltpu.VMEM((LANES, cells), BF16), pltpu.VMEM((LANES, cells), BF16),
            wide, wide,
            pltpu.VMEM((LIFT_AT, cells), BF16), pltpu.VMEM((LIFT_AT, cells), BF16),
            pltpu.VMEM((3 * channels, cells), F32),
            pltpu.VMEM((channels, cells), F32),
            pltpu.VMEM((3 * channels, cells), BF16), pltpu.VMEM((3 * channels, cells), BF16),
        ],
        compiler_params=pltpu.CompilerParams(vmem_limit_bytes=48 * 2**20),
        cost_estimate=pl.CostEstimate(
            flops=5 * 10**9, bytes_accessed=4 * 2**20, transcendentals=2**18
        ),
        name="surrogate",
    )(owners, fields, target, lift, mix, mix_back, out_w)


def reduce_kernel(n_row, n_col, packed, out, loss, got, total, pieces, *sems):
    a_send, a_recv, b_send, b_recv, c_send, c_recv, d_send, d_recv = sems
    row, col = lax.axis_index("gx"), lax.axis_index("sec")
    per = total.shape[0]
    piece = per // n_row

    def along_col(d):
        return (row, lax.rem(col + d, n_col))

    def along_row(d):
        return (lax.rem(row + d, n_row), col)

    barrier = pltpu.get_barrier_semaphore()
    for d in range(1, n_col):
        pl.semaphore_signal(barrier, inc=1, device_id=along_col(d), device_id_type=MESH)
    for d in range(1, n_row):
        pl.semaphore_signal(barrier, inc=1, device_id=along_row(d), device_id_type=MESH)
    pl.semaphore_wait(barrier, n_col + n_row - 2)

    def send(source, target, sent, received, where):
        copy = pltpu.make_async_remote_copy(
            src_ref=source, dst_ref=target, send_sem=sent, recv_sem=received,
            device_id=where, device_id_type=MESH,
        )
        copy.start()
        return copy

    copies = [
        send(packed.at[along_col(d)[1]], got.at[d - 1], a_send.at[d - 1], a_recv.at[d - 1], along_col(d))
        for d in range(1, n_col)
    ]
    for copy in copies:
        copy.wait_recv()
    total[...] = packed[col, :per] + sum(got[d, :per] for d in range(n_col - 1))
    loss[...] = packed[col, per] + sum(got[d, per] for d in range(n_col - 1))
    for copy in copies:
        copy.wait_send()

    def mine(at):
        return pl.ds(at * piece, piece)

    copies = [
        send(total.at[mine(along_row(d)[0])], pieces.at[d - 1], b_send.at[d - 1], b_recv.at[d - 1], along_row(d))
        for d in range(1, n_row)
    ]
    for copy in copies:
        copy.wait_recv()
    out[col, mine(row)] = total[mine(row)] + sum(pieces[d] for d in range(n_row - 1))
    for copy in copies:
        copy.wait_send()
    copies = [
        send(out.at[col, mine(row)], out.at[col, mine(row)], c_send.at[d - 1], c_recv.at[d - 1], along_row(d))
        for d in range(1, n_row)
    ]
    for copy in copies:
        copy.wait()
    copies = [
        send(out.at[col], out.at[col], d_send.at[d - 1], d_recv.at[d - 1], along_col(d))
        for d in range(1, n_col)
    ]
    for copy in copies:
        copy.wait()


def reduced(packed, n_row, n_col):
    per = packed.shape[1] - 1
    tile = (SUBLANES, LANES)
    vmem = pl.BlockSpec(memory_space=pltpu.VMEM)
    dma = pltpu.SemaphoreType.DMA
    return pl.pallas_call(
        functools.partial(reduce_kernel, n_row, n_col),
        out_shape=(
            jax.ShapeDtypeStruct((n_col, per) + tile, F32),
            jax.ShapeDtypeStruct(tile, F32),
        ),
        in_specs=[vmem],
        out_specs=(vmem, vmem),
        scratch_shapes=[
            pltpu.VMEM((n_col - 1, per + 1) + tile, F32),
            pltpu.VMEM((per,) + tile, F32),
            pltpu.VMEM((n_row - 1, per // n_row) + tile, F32),
        ]
        + [dma((n - 1,)) for n in (n_col, n_col, n_row, n_row, n_row, n_row, n_col, n_col)],
        compiler_params=pltpu.CompilerParams(collective_id=1, has_side_effects=True),
        cost_estimate=pl.CostEstimate(flops=2**20, bytes_accessed=2**22, transcendentals=0),
        name="reduced",
    )(packed)


def lift_columns():
    return [lift_row(tap) + channel for tap in range(9) for channel in range(2)]


def train(stacked, owners, lift_weight, mix_weight, out_weight, n_row, n_col):
    channels = out_weight.shape[1]
    count = stacked.shape[0]
    cells = count * 512
    flat = stacked.reshape(count // 2, 2, 3, 8, 64).transpose(2, 0, 3, 1, 4).reshape(3, cells)
    zero2, zero6 = jnp.zeros((2, cells), F32), jnp.zeros((6, cells), F32)
    fields = jnp.concatenate([flat[0:2], zero6, zero2, zero2, flat[0:2], zero2], axis=0)
    taps = mix_weight.reshape(channels, channels, 3, 9)
    mix = taps.transpose(2, 0, 3, 1).reshape(3 * channels, 9 * channels)
    mix_back = taps[:, :, ::-1, ::-1].transpose(2, 1, 3, 0).reshape(3 * channels, 9 * channels)
    lifted = lift_weight.reshape(channels, 2, 3, 9).transpose(2, 0, 3, 1).reshape(3 * channels, 9, 2)
    early = jnp.pad(lifted[:, :5], ((0, 0), (0, 0), (0, 2)))
    late = jnp.pad(lifted[:, 5:], ((0, 0), (0, 1), (0, 2)))
    lift = jnp.concatenate([early, late], axis=2).reshape(3 * channels, 40)
    lift = jnp.pad(lift, ((0, 0), (0, 8)))
    column_tiles = PACKED // LANES
    row_tiles = 3 * channels // SUBLANES
    used = column_tiles * row_tiles
    per = n_row * (-(-used // (n_col * n_row)))
    packed = surrogate(
        owners, fields, flat[2:3], lift, mix, mix_back, out_weight.reshape(channels, 1), n_col, per
    )
    summed, loss = reduced(packed, n_row, n_col)
    grads = summed.reshape(n_col * per, SUBLANES, LANES)[:used]
    grads = grads.reshape(column_tiles, 3 * channels, LANES)
    wide = grads.transpose(1, 0, 2).reshape(3, channels, PACKED)
    mix_grad = wide[:, :, :LIFT_AT].reshape(3, channels, 9, channels)
    mix_grad = mix_grad.transpose(1, 3, 0, 2).reshape(channels, 27 * channels)
    lift_part = wide[:, :, LIFT_AT : LIFT_AT + 40].reshape(3, channels, 5, 2, 4)
    early, late = lift_part[:, :, :, 0, :2], lift_part[:, :, :4, 1, :2]
    lift_grad = jnp.concatenate([early, late], axis=2)
    lift_grad = lift_grad.transpose(1, 3, 0, 2).reshape(channels, 54)
    out_grad = wide[0, :, PACKED - 1].reshape(1, channels)
    return lift_grad, mix_grad, out_grad, loss[:1, :1]


def add_rim(values):
    return padded(values, (("gx", 1), ("sec", 2)), 1)


def on_device(
    scalar_field, diffusivity, corner_x, corner_y, patch_owner, lift_weight, mix_weight, out_weight
):
    first_step = advance(add_rim(scalar_field), diffusivity)
    advanced = advance(add_rim(first_step), diffusivity)
    change = advanced - first_step
    fields = jnp.stack([first_step, diffusivity, change])
    depth = fields.shape[1]
    per_device = corner_x.shape[2]
    row_index = lax.axis_index("gx")
    column_index = lax.axis_index("sec")
    zero = jnp.zeros((), jnp.int32)
    my_corner_x = corner_x[0, 0]
    corners_y = corner_y[:, 0]
    my_corner_y = lax.dynamic_index_in_dim(corners_y, row_index, 0, keepdims=False)
    piece_size = (3, depth, depth, depth)
    pieces = []
    following = from_behind(fields[:, :, :depth], "gx", -1)
    joined = jnp.concatenate([fields, following], axis=2)
    for number in range(per_device):
        pieces.append(
            lax.dynamic_slice(
                joined, (zero, zero, my_corner_x[number], my_corner_y[number]), piece_size
            )
        )
    stacked = jnp.stack(pieces)
    my_owners = lax.dynamic_index_in_dim(patch_owner[0], column_index, 0, keepdims=False)
    trained = train(
        stacked, my_owners, lift_weight, mix_weight, out_weight,
        lax.axis_size("gx"), lax.axis_size("sec"),
    )
    return (advanced,) + trained


def solution(mesh):
    in_specs = (
        P(None, "gx", "sec"),
        P(None, "gx", "sec"),
        P("gx", "sec", None),
        P(None, "sec", None),
        P("gx", None, None),
        P(),
        P(),
        P(),
    )
    out_specs = (P(None, "gx", "sec"), P(), P(), P(), P("gx", "sec"))
    return jax.shard_map(
        on_device, mesh=mesh, in_specs=in_specs, out_specs=out_specs, check_vma=False
    )
```
